32 devices in a mesh: expert: 4 (over y, core), dp: 8 (over z, x).
Axes of the slice: x: 2, y: 2, z: 4, core: 2. Of those that a mesh axis runs over, the one named last changes fastest.
Arguments:
- out_grad: bfloat16 [4096, 2048], P(('dp', 'expert')), parts along dimension 0, may hold values from -6 to 6
- route_ids: int32 [4096, 8], P(('dp', 'expert')), parts along dimension 0, may hold values from 0 to 31, as said below
- combine: float32 [4096, 8], P(('dp', 'expert')), parts along dimension 0, may hold values from 0.25 to 1
- row_lists: int32 [16, 4, 192], P('dp', None, 'expert'), parts along dimension 0, may hold values from -1 to 127, as said below
- saved_inputs: bfloat16 [16, 4, 192, 2048], P('dp', 'expert'), parts along dimension 0, may hold values from -6 to 6
- gate_weight: bfloat16 [4, 2048, 384], P('expert'), may hold values from -0.125 to 0.125
- up_weight: bfloat16 [4, 2048, 384], P('expert'), may hold values from -0.125 to 0.125
- down_weight: bfloat16 [4, 384, 2048], P('expert'), may hold values from -0.3125 to 0.3125
Outputs:
- input_grad: bfloat16 [4096, 2048], P(('dp', 'expert')), parts along dimension 0
The draws below stay inside these ranges and needn't reach their ends.
There are 8 independent parts, one for each index of `dp`. The reference program is written for one: setup_inputs(seed, part) draws one part's arguments, and reference() takes and returns one part's arrays. A program takes and returns all parts, laid end to end along the dimension named above; an argument that names none is the same for every part. Nothing has to cross between parts.
Inputs may be any that keep to these rules, and one draw needn't show every extreme that they name: `route_ids`: each row names 8 different experts; expert e below 4 is held at index e of the expert axis, the others are outside this window. `row_lists`: entry [m, e, s * 48 + p] is -1 (empty) or the index, among the 128 tokens at index s of the expert axis, of a token of micro-batch m (index divided by 64 equals m) whose route_ids name e. Within each aligned block of 48 entries the indices rise and empty entries come last; a token stands at most once in the lists of one expert. Tokens naming e beyond 48 from one index in one micro-batch are left out. In every micro-batch some expert's block has all 192 entries filled.
All inputs are finite; a program needn't handle non-finite values.
Results may differ from the reference program's by a relative error of at most 0.0062.
Values may be sent and summed in bfloat16 or wider, within the bound.
A program may use at most 64 MiB of HBM per device.

```python
import jax
import jax.numpy as jnp
from jax import lax

D = 2048
FF = 384
TOP = 8
MB = 2
CAP = 192
TOK_DEV = 128
EXPERTS = 4
EXPERTS_ALL = 32
PAIR = 48
TOKENS = 512


def route_plan(key):
    key = jax.random.fold_in(key, 11)
    key_score, key_hot, key_shift = jax.random.split(key, 3)
    half_batch = TOK_DEV // 2
    noise = jax.random.randint(key_score, (TOKENS, EXPERTS_ALL), 0, 1 << 20)
    labels = jnp.arange(EXPERTS_ALL, dtype=jnp.int32)
    scores = noise * EXPERTS_ALL + labels[None, :]
    hot_expert = jax.random.randint(key_hot, (MB,), 0, EXPERTS)
    offset = jax.random.randint(key_shift, (MB, EXPERTS), 0, half_batch)
    token_index = jnp.arange(TOKENS, dtype=jnp.int32)
    source = token_index // TOK_DEV
    local_index = token_index % TOK_DEV
    batch_of = local_index // half_batch
    inside = local_index % half_batch
    chosen = (inside + offset[batch_of, source]) % half_batch < PAIR
    boosted = jnp.logical_and(chosen[:, None], labels[None, :] == hot_expert[batch_of][:, None])
    scores = scores + boosted.astype(jnp.int32) * (1 << 28)
    routing = lax.top_k(scores, TOP)[1].astype(jnp.int32)
    window_ids = jnp.arange(EXPERTS, dtype=jnp.int32)
    member = jnp.any(routing[:, :, None] == window_ids[None, None, :], axis=1).astype(jnp.int32)
    member = member.reshape(EXPERTS, MB, half_batch, EXPERTS)
    running = jnp.cumsum(member, axis=2)
    places = jnp.arange(PAIR, dtype=jnp.int32)
    before = jnp.sum((running[:, :, :, None, :] <= places[None, None, None, :, None]).astype(jnp.int32), axis=2)
    totals = running[:, :, half_batch - 1, :]
    occupied = places[None, None, :, None] < totals[:, :, None, :]
    first_slot = (jnp.arange(MB, dtype=jnp.int32) * half_batch)[None, :, None, None]
    entries = jnp.where(occupied, before + first_slot, -1).astype(jnp.int32)
    slot_lists = jnp.transpose(entries, (1, 3, 0, 2)).reshape(MB, EXPERTS, CAP)
    return (routing, slot_lists)


def draw_route_ids(key, part):
    return route_plan(key)[0]


def draw_row_lists(key, part):
    return route_plan(key)[1]


def level_of(rng, dims, cuts, low, largest):
    level, own = 1.0, jax.random.fold_in(rng, 6)
    for dim, parts in cuts:
        draws = jnp.exp(jax.random.uniform(jax.random.fold_in(own, dim), (parts,), jnp.float32, low / len(cuts), largest / len(cuts)))
        level = level * jnp.repeat(draws, dims[dim] // parts).reshape([-1 if axis == dim else 1 for axis in range(len(dims))])
    return level


def normal_values(own_key, extent, deviation, limit, cuts=(), held_as=jnp.bfloat16):
    drawn = jax.random.normal(own_key, extent, jnp.float32) * deviation
    if len(cuts) > 0:
        drawn = level_of(own_key, extent, cuts, -0.22, 0.18) * drawn
    return jnp.clip(drawn, min=-limit, max=limit).astype(held_as)


def setup_inputs(seed: int = 0, part: int = 0) -> dict:
    keys = jax.random.split(jax.random.key(seed), 9)
    own_keys = jax.random.split(jax.random.fold_in(keys[8], part), 9)
    return {
        "out_grad": normal_values(own_keys[0], (TOKENS, D), 1.0, 6.0, ((0, 4),)),
        "route_ids": draw_route_ids(jax.random.fold_in(jax.random.fold_in(keys[8], part), 71), part),
        "combine": jnp.clip(0.25 + 0.75 * jax.random.uniform(own_keys[2], (TOKENS, TOP), jnp.float32) ** level_of(own_keys[2], (TOKENS, TOP), ((0, 4),), -0.2, 0.2), 0.25, 1.0),
        "row_lists": draw_row_lists(jax.random.fold_in(jax.random.fold_in(keys[8], part), 71), part),
        "saved_inputs": normal_values(own_keys[4], (MB, EXPERTS, CAP, D), 1.0, 6.0, ((1, 4),)),
        "gate_weight": normal_values(keys[5], (EXPERTS, D, FF), D ** -0.5, 0.125, ((0, 4),)),
        "up_weight": normal_values(keys[6], (EXPERTS, D, FF), D ** -0.5, 0.125, ((0, 4),)),
        "down_weight": normal_values(keys[7], (EXPERTS, FF, D), FF ** -0.5, 0.3125, ((0, 4),)),
    }


def expert_backward(saved_rows, weighted, gate_weight, up_weight, down_weight):
    contract = (((1,), (1,)), ((), ()))
    gate_value = jnp.dot(saved_rows, gate_weight, preferred_element_type=jnp.float32)
    up_value = jnp.dot(saved_rows, up_weight, preferred_element_type=jnp.float32)
    grad_hidden = lax.dot_general(weighted, down_weight, contract, preferred_element_type=jnp.float32)
    sigmoid_gate = jax.nn.sigmoid(gate_value)
    silu_gate = gate_value * sigmoid_gate
    grad_gate = (grad_hidden * up_value * sigmoid_gate * (1.0 + gate_value * (1.0 - sigmoid_gate))).astype(jnp.bfloat16)
    grad_up = (grad_hidden * silu_gate).astype(jnp.bfloat16)
    slot_grad = lax.dot_general(grad_gate, gate_weight, contract, preferred_element_type=jnp.float32)
    slot_grad = slot_grad + lax.dot_general(grad_up, up_weight, contract, preferred_element_type=jnp.float32)
    return slot_grad.astype(jnp.bfloat16)


def reference(out_grad, route_ids, combine, row_lists, saved_inputs, gate_weight, up_weight, down_weight):
    accumulated = jnp.zeros((TOKENS, D), jnp.float32)
    slot_source = (jnp.arange(CAP, dtype=jnp.int32) // PAIR).astype(jnp.int32)
    for batch_index in range(MB):
        def per_expert(expert_index):
            slot_entries = row_lists[batch_index, expert_index]
            occupied = slot_entries >= 0
            token_index = jnp.where(occupied, slot_source * TOK_DEV + slot_entries, 0).astype(jnp.int32)
            named = route_ids[token_index] == expert_index
            token_weight = jnp.sum(jnp.where(named, combine[token_index], jnp.float32(0.0)), axis=1)
            slot_weight = jnp.where(occupied, token_weight, jnp.float32(0.0))
            weighted = (out_grad[token_index].astype(jnp.float32) * slot_weight[:, None]).astype(jnp.bfloat16)
            slot_grad = expert_backward(saved_inputs[batch_index, expert_index], weighted,
                                        gate_weight[expert_index], up_weight[expert_index], down_weight[expert_index])
            return token_index, jnp.where(occupied[:, None], slot_grad.astype(jnp.float32), jnp.float32(0.0))

        index_all, grads_all = lax.map(per_expert, jnp.arange(EXPERTS, dtype=jnp.int32))
        accumulated = accumulated.at[index_all.reshape(-1)].add(grads_all.reshape(-1, D))
    return accumulated.astype(jnp.bfloat16)
```

```python
import functools

import jax
import jax.numpy as jnp
from jax import lax
from jax.experimental import pallas as pl
from jax.experimental.pallas import tpu as pltpu
from jax.sharding import PartitionSpec as P

MESH = pl.DeviceIdType.MESH
BF16 = jnp.bfloat16
F32 = jnp.float32
CORES = 2


def kernel(
    n,
    og_ref, route_ref, combine_ref, lists_ref, saved_ref, gate_ref, up_ref, down_ref,
    out_ref,
    og, saved, gate, up, down, meta_out, meta_in, tokens_in, gate_factor, up_factor,
    part, part_in, back_out, back_in, own_sum,
    load_sem, meta_send, meta_recv, og_send, og_recv, part_send, part_recv, back_send, back_recv,
):
    chips = n // CORES
    batches, experts, width = lists_ref.shape
    slots = saved.shape[1]
    rows = og.shape[3]
    hidden = down.shape[0]
    lanes = meta_in.shape[3]
    me = lax.axis_index("expert")
    chip, core = me // CORES, me % CORES
    other = 1 - core

    def device(d, k):
        return {"expert": lax.rem(chip + d, chips) * CORES + (core if k == 0 else other)}

    partner = device(0, 1)

    def remote(src, dst, send, recv, target):
        return pltpu.make_async_remote_copy(
            src_ref=src, dst_ref=dst, send_sem=send, recv_sem=recv, device_id=target, device_id_type=MESH
        )

    barrier = pltpu.get_barrier_semaphore()
    places = [(d, k) for d in range(chips) for k in range(CORES)]
    others = places[1:]
    for d, k in others:
        pl.semaphore_signal(barrier, inc=1, device_id=device(d, k), device_id_type=MESH)

    loads = [
        pltpu.make_async_copy(saved_ref.at[:, 0], saved, load_sem.at[0]),
        pltpu.make_async_copy(gate_ref.at[0], gate, load_sem.at[1]),
        pltpu.make_async_copy(up_ref.at[0], up, load_sem.at[2]),
        pltpu.make_async_copy(down_ref.at[0], down, load_sem.at[3]),
    ]
    own = [
        pltpu.make_async_copy(og_ref.at[pl.ds(m * rows, rows)], og.at[0, 0, m], load_sem.at[4 + m])
        for m in range(batches)
    ]
    for copy in loads + own:
        copy.start()

    owned = og_ref.shape[0]
    route = route_ref[...]
    combine = combine_ref[...]
    lane = lax.broadcasted_iota(jnp.int32, (1, lanes), 1)
    mine = jnp.logical_and(lane >= me * width, lane < (me + 1) * width)
    pad = [jnp.full((1, lanes - slots), -1, jnp.int32)] if lanes > slots else []
    for d, k in places:
        target = device(d, k)["expert"]
        weight_row = jnp.sum(jnp.where(route == target, combine, 0.0), axis=0, keepdims=True)
        where = meta_in if (d, k) == (0, 0) else meta_out
        where[d, k, 0:1, 0:owned] = weight_row
        for m in range(batches):
            entries = lists_ref[m, pl.ds(target, 1), :]
            tiled = jnp.concatenate([entries] * experts + pad, axis=1)
            where[d, k, 1 + m : 2 + m, :] = jnp.where(mine, tiled, -1).astype(F32)

    pl.semaphore_wait(barrier, n - 1)

    sends = []

    def launch(copy):
        copy.start()
        sends.append(copy)
        return copy

    metas = {
        (d, k): launch(
            remote(meta_out.at[d, k], meta_in.at[d, k], meta_send.at[d, k], meta_recv.at[d, k], device(d, k))
        )
        for d, k in others
    }
    arrivals = {}
    for m in range(batches):
        part_rows = og_ref.at[pl.ds(m * rows, rows)]
        for d in range(1, chips):
            arrivals[d, 0, m] = launch(
                remote(part_rows, og.at[d, 0, m], og_send.at[d, 0, m], og_recv.at[d, 0, m], device(d, 0))
            )
        arrivals[0, 1, m] = launch(
            remote(part_rows, og.at[0, 1, m], og_send.at[0, 1, m], og_recv.at[0, 1, m], partner)
        )

    for place in others:
        metas[place].wait_recv()
    loads[0].wait()
    token = lax.broadcasted_iota(jnp.int32, (rows, slots), 0)
    for m in range(batches):
        wanted = (token + m * rows).astype(F32)
        for i, (d, k) in enumerate(places):
            listed = meta_in[d, k, 1 + m : 2 + m, 0:slots]
            select = jnp.where(listed == wanted, 1.0, 0.0).astype(BF16)
            tokens_in[m, i * rows : (i + 1) * rows, :] = jnp.dot(
                select, saved[m], preferred_element_type=F32
            ).astype(BF16)
    loads[1].wait()
    loads[2].wait()
    eye = lax.broadcasted_iota(jnp.int32, (rows, rows), 0) == lax.broadcasted_iota(
        jnp.int32, (rows, rows), 1
    )
    for m in range(batches):
        gate_value = jnp.dot(tokens_in[m], gate[...], preferred_element_type=F32)
        up_value = jnp.dot(tokens_in[m], up[...], preferred_element_type=F32)
        sigmoid = jax.nn.sigmoid(gate_value)
        columns = []
        for d, k in places:
            weight_row = meta_in[d, k, 0:1, m * rows : (m + 1) * rows]
            columns.append(
                jnp.sum(jnp.where(eye, weight_row, 0.0), axis=1, keepdims=True)
            )
        weight = jnp.concatenate(columns, axis=0)
        gate_factor[m] = weight * (up_value * sigmoid * (1.0 + gate_value * (1.0 - sigmoid)))
        up_factor[m] = weight * (gate_value * sigmoid)

    contract = (((1,), (1,)), ((), ()))

    def slot_grad(m, d, k, count=1):
        first = (d * CORES + k) * rows
        span = slice(first, first + count * rows)
        grads = og[d, k, m] if count == 1 else jnp.concatenate([og[d, k + j, m] for j in range(count)], axis=0)
        grad_hidden = lax.dot_general(grads, down[...], contract, preferred_element_type=F32)
        grad_gate = (grad_hidden * gate_factor[m, span, :]).astype(BF16)
        grad_up = (grad_hidden * up_factor[m, span, :]).astype(BF16)
        return lax.dot_general(grad_gate, gate[...], contract, preferred_element_type=F32) + lax.dot_general(
            grad_up, up[...], contract, preferred_element_type=F32
        )

    loads[3].wait()
    partials = {}
    for m in range(batches):
        own[m].wait()
        arrivals[0, 1, m].wait_recv()
        both = slot_grad(m, 0, 0, 2)
        own_sum[m] = both[0:rows]
        part[0, m] = both[rows : 2 * rows].astype(BF16)
        partials[0, m] = launch(
            remote(part.at[0, m], part_in.at[0, m], part_send.at[0, m], part_recv.at[0, m], partner)
        )

    backs = {}
    for m in range(batches):
        for d in range(1, chips):
            arrivals[d, 0, m].wait_recv()
            arrivals[d, 1, m] = launch(
                remote(og.at[d, 0, m], og.at[d, 1, m], og_send.at[d, 1, m], og_recv.at[d, 1, m], partner)
            )
        for d in range(1, chips):
            arrivals[d, 1, m].wait_recv()
            both = slot_grad(m, d, 0, 2)
            part[d, m] = both[rows : 2 * rows].astype(BF16)
            partials[d, m] = launch(
                remote(part.at[d, m], part_in.at[d, m], part_send.at[d, m], part_recv.at[d, m], partner)
            )
            mine_sum = both[0:rows].astype(BF16).astype(F32)
            partials[d, m].wait_recv()
            back_out[d, m] = (mine_sum + part_in[d, m].astype(F32)).astype(BF16)
            backs[d, m] = launch(
                remote(
                    back_out.at[d, m], back_in.at[d, m], back_send.at[d, m], back_recv.at[d, m],
                    device(chips - d, 0),
                )
            )

    for m in range(batches):
        partials[0, m].wait_recv()
        own_sum[m] = own_sum[m] + part_in[0, m].astype(F32)
    for m in range(batches):
        total = own_sum[m]
        for d in range(1, chips):
            backs[d, m].wait_recv()
            total = total + back_in[d, m].astype(F32)
        out_ref[m * rows : (m + 1) * rows, :] = total.astype(out_ref.dtype)
    for copy in sends:
        copy.wait_send()


def on_device(
    out_grad, route_ids, combine, row_lists, saved_inputs, gate_weight, up_weight, down_weight
):
    n = lax.axis_size("expert")
    chips = n // CORES
    batches = row_lists.shape[0]
    owned, width = out_grad.shape
    rows = owned // batches
    slots = saved_inputs.shape[2]
    hidden = gate_weight.shape[2]
    lanes = max(-(-slots // 128), -(-owned // 128)) * 128
    meta_rows = -(-(1 + batches) // 8) * 8
    hbm = pl.BlockSpec(memory_space=pl.ANY)
    vmem = pl.BlockSpec(memory_space=pltpu.VMEM)
    dma = pltpu.SemaphoreType.DMA
    return pl.pallas_call(
        functools.partial(kernel, n),
        out_shape=jax.ShapeDtypeStruct(out_grad.shape, out_grad.dtype),
        in_specs=[hbm, vmem, vmem, vmem, hbm, hbm, hbm, hbm],
        out_specs=vmem,
        scratch_shapes=[
            pltpu.VMEM((chips, CORES, batches, rows, width), BF16),
            pltpu.VMEM((batches, slots, width), BF16),
            pltpu.VMEM((width, hidden), BF16),
            pltpu.VMEM((width, hidden), BF16),
            pltpu.VMEM((hidden, width), BF16),
            pltpu.VMEM((chips, CORES, meta_rows, lanes), F32),
            pltpu.VMEM((chips, CORES, meta_rows, lanes), F32),
            pltpu.VMEM((batches, n * rows, width), BF16),
            pltpu.VMEM((batches, n * rows, hidden), F32),
            pltpu.VMEM((batches, n * rows, hidden), F32),
            pltpu.VMEM((chips, batches, rows, width), BF16),
            pltpu.VMEM((chips, batches, rows, width), BF16),
            pltpu.VMEM((chips, batches, rows, width), BF16),
            pltpu.VMEM((chips, batches, rows, width), BF16),
            pltpu.VMEM((batches, rows, width), F32),
            dma((4 + batches,)),
            dma((chips, CORES)),
            dma((chips, CORES)),
            dma((chips, CORES, batches)),
            dma((chips, CORES, batches)),
            dma((chips, batches)),
            dma((chips, batches)),
            dma((chips, batches)),
            dma((chips, batches)),
        ],
        compiler_params=pltpu.CompilerParams(
            collective_id=0, has_side_effects=True, vmem_limit_bytes=60 * 1024 * 1024
        ),
    )(out_grad, route_ids.T, combine.T, row_lists, saved_inputs, gate_weight, up_weight, down_weight)


def solution(mesh):
    return jax.shard_map(
        on_device,
        mesh=mesh,
        in_specs=(
            P(("dp", "expert"), None),
            P(("dp", "expert"), None),
            P(("dp", "expert"), None),
            P("dp", None, "expert"),
            P("dp", "expert", None, None),
            P("expert", None, None),
            P("expert", None, None),
            P("expert", None, None),
        ),
        out_specs=P(("dp", "expert"), None),
        check_vma=False,
    )
```

```python
import functools

import jax
import jax.numpy as jnp
from jax import lax
from jax.experimental import pallas as pl
from jax.experimental.pallas import tpu as pltpu
from jax.sharding import PartitionSpec as P

MESH = pl.DeviceIdType.MESH
BF16 = jnp.bfloat16
F32 = jnp.float32
CORES = 2


def kernel(
    n, splits,
    og_ref, route_ref, combine_ref, lists_ref, saved_ref, gate_ref, up_ref, down_ref,
    out_ref,
    og, saved, gate, up, down, meta_out, meta_in, tokens_in, gate_factor, up_factor,
    part, part_own, part_in, back_in, own_sum,
    down_t, pair_t,
    load_sem, meta_send, meta_recv, og_send, og_recv, part_send, part_recv, back_send, back_recv,
):
    chips = n // CORES
    batches, experts, width = lists_ref.shape
    slots = saved.shape[1]
    rows = og.shape[3]
    hidden = down.shape[0]
    lanes = meta_in.shape[3]
    me = lax.axis_index("expert")
    chip, core = me // CORES, me % CORES
    other = 1 - core

    def device(d, k):
        return {"expert": lax.rem(chip + d, chips) * CORES + (core if k == 0 else other)}

    partner = device(0, 1)

    def remote(src, dst, send, recv, target):
        return pltpu.make_async_remote_copy(
            src_ref=src, dst_ref=dst, send_sem=send, recv_sem=recv, device_id=target, device_id_type=MESH
        )

    barrier = pltpu.get_barrier_semaphore()
    places = [(d, k) for d in range(chips) for k in range(CORES)]
    others = places[1:]
    for d, k in others:
        pl.semaphore_signal(barrier, inc=1, device_id=device(d, k), device_id_type=MESH)

    loads = [
        pltpu.make_async_copy(saved_ref.at[:, 0], saved, load_sem.at[0]),
        pltpu.make_async_copy(gate_ref.at[0], gate, load_sem.at[1]),
        pltpu.make_async_copy(up_ref.at[0], up, load_sem.at[2]),
        pltpu.make_async_copy(down_ref.at[0], down, load_sem.at[3]),
    ]
    own = [
        pltpu.make_async_copy(og_ref.at[pl.ds(m * rows, rows)], og.at[0, 0, m], load_sem.at[4 + m])
        for m in range(batches)
    ]
    for copy in loads + own:
        copy.start()

    owned = og_ref.shape[0]
    route = route_ref[...]
    combine = combine_ref[...]
    lane = lax.broadcasted_iota(jnp.int32, (1, lanes), 1)
    mine = jnp.logical_and(lane >= me * width, lane < (me + 1) * width)
    pad = [jnp.full((1, lanes - slots), -1, jnp.int32)] if lanes > slots else []
    for d, k in places:
        target = device(d, k)["expert"]
        weight_row = jnp.sum(jnp.where(route == target, combine, 0.0), axis=0, keepdims=True)
        where = meta_in if (d, k) == (0, 0) else meta_out
        where[d, k, 0:1, 0:owned] = weight_row
        for m in range(batches):
            entries = lists_ref[m, pl.ds(target, 1), :]
            tiled = jnp.concatenate([entries] * experts + pad, axis=1)
            where[d, k, 1 + m : 2 + m, :] = jnp.where(mine, tiled, -1).astype(F32)

    pl.semaphore_wait(barrier, n - 1)

    sends = []

    def launch(copy):
        copy.start()
        sends.append(copy)
        return copy

    metas = {
        (d, k): launch(
            remote(meta_out.at[d, k], meta_in.at[d, k], meta_send.at[d, k], meta_recv.at[d, k], device(d, k))
        )
        for d, k in others
    }
    distances = range(1, chips)
    pieces = []
    for m in range(batches):
        cuts = splits[m]
        pieces += [(m, pl.ds(i * (rows // cuts), rows // cuts), i * (rows // cuts)) for i in range(cuts)]
    numbered = list(enumerate(pieces))
    arrivals = {}
    for p, (m, span, first) in numbered:
        for d in distances:
            arrivals[d, 0, p] = launch(
                remote(
                    og_ref.at[pl.ds(m * rows + first, span.size)], og.at[d, 0, m, span],
                    og_send.at[d, 0, p], og_recv.at[d, 0, p], device(d, 0),
                )
            )
        if first == 0:
            arrivals[0, 1, m] = launch(
                remote(
                    og_ref.at[pl.ds(m * rows, rows)], og.at[0, 1, m],
                    og_send.at[0, 1, m], og_recv.at[0, 1, m], partner,
                )
            )

    token = lax.broadcasted_iota(jnp.int32, (rows, slots), 0)
    eye = lax.broadcasted_iota(jnp.int32, (rows, rows), 0) == lax.broadcasted_iota(
        jnp.int32, (rows, rows), 1
    )

    def factors(m):
        wanted = (token + m * rows).astype(F32)
        columns = []
        for i, (d, k) in enumerate(places):
            listed = meta_in[d, k, 1 + m : 2 + m, 0:slots]
            select = jnp.where(listed == wanted, 1.0, 0.0).astype(BF16)
            tokens_in[m, i * rows : (i + 1) * rows, :] = jnp.dot(
                select, saved[m], preferred_element_type=F32
            ).astype(BF16)
            weight_row = meta_in[d, k, 0:1, m * rows : (m + 1) * rows]
            columns.append(jnp.sum(jnp.where(eye, weight_row, 0.0), axis=1, keepdims=True))
        if m == 0:
            loads[1].wait()
            loads[2].wait()
        gate_value = jnp.dot(tokens_in[m], gate[...], preferred_element_type=F32)
        up_value = jnp.dot(tokens_in[m], up[...], preferred_element_type=F32)
        sigmoid = jax.nn.sigmoid(gate_value)
        weight = jnp.concatenate(columns, axis=0)
        gate_factor[m] = weight * (up_value * sigmoid * (1.0 + gate_value * (1.0 - sigmoid)))
        up_factor[m] = weight * (gate_value * sigmoid)


    def slot_grad(m, d, first, count):
        starts = [(d * CORES + k) * rows + first for k in range(CORES)]

        def both_cores(ref):
            return jnp.concatenate([ref[m, i : i + count, :] for i in starts], axis=0)

        grads = jnp.concatenate([og[d, k, m, first : first + count, :] for k in range(CORES)], axis=0)
        grad_hidden = jnp.dot(grads, down_t[...], preferred_element_type=F32)
        grad_gate = (grad_hidden * both_cores(gate_factor)).astype(BF16)
        grad_up = (grad_hidden * both_cores(up_factor)).astype(BF16)
        pair = jnp.concatenate([grad_gate, grad_up], axis=1)
        return jnp.dot(pair, pair_t[...], preferred_element_type=F32)

    partials, backs = {}, {}

    def exchange(p, m, d, span):
        copy = remote(
            part.at[d, m, span], part_in.at[d, m, span], part_send.at[d, p], part_recv.at[d, p], partner
        )
        partials[d, p] = launch(copy)

    def near(m):
        own[m].wait()
        arrivals[0, 1, m].wait_recv()
        both = slot_grad(m, 0, 0, rows)
        part[0, m] = both[rows : 2 * rows].astype(BF16)
        exchange(m, m, 0, pl.ds(0, rows))
        own_sum[m] = both[0:rows]

    def relay(p, d):
        m, span, first = pieces[p]
        arrivals[d, 0, p].wait_recv()
        arrivals[d, 1, p] = launch(
            remote(
                og.at[d, 0, m, span], og.at[d, 1, m, span], og_send.at[d, 1, p], og_recv.at[d, 1, p], partner
            )
        )

    def far(p, d):
        m, span, first = pieces[p]
        count = span.size
        arrivals[d, 1, p].wait_recv()
        both = slot_grad(m, d, first, count)
        part[d, m, first : first + count, :] = both[count : 2 * count].astype(BF16)
        exchange(p, m, d, span)
        part_own[d, m, first : first + count, :] = both[0:count].astype(BF16)

    def give_back(p, d):
        m, span, first = pieces[p]
        here = slice(first, first + span.size)
        partials[d, p].wait_recv()
        part_own[d, m, here, :] = (part_own[d, m, here, :].astype(F32) + part_in[d, m, here, :].astype(F32)).astype(
            BF16
        )
        backs[d, p] = launch(
            remote(
                part_own.at[d, m, span], back_in.at[d, m, span], back_send.at[d, p], back_recv.at[d, p],
                device(chips - d, 0),
            )
        )

    for place in others:
        metas[place].wait_recv()
    loads[0].wait()
    factors(0)
    loads[3].wait()
    down_t[...] = down[...].T
    pair_t[0:hidden, :] = gate[...].T
    pair_t[hidden : 2 * hidden, :] = up[...].T
    near(0)
    for p, (m, span, first) in numbered:
        for d in distances:
            relay(p, d)
        if p > 0:
            for d in distances:
                give_back(p - 1, d)
        if first + span.size == rows and m + 1 < batches:
            factors(m + 1)
        for d in distances:
            far(p, d)
    for m in range(1, batches):
        near(m)
    for d in distances:
        give_back(len(pieces) - 1, d)
    for m in range(batches):
        partials[0, m].wait_recv()
        own_sum[m] = own_sum[m] + part_in[0, m].astype(F32)
    for p, (m, span, first) in numbered:
        here = slice(first, first + span.size)
        total = own_sum[m, here, :]
        for d in distances:
            backs[d, p].wait_recv()
            total = total + back_in[d, m, here, :].astype(F32)
        out_ref[m * rows + first : m * rows + first + span.size, :] = total.astype(out_ref.dtype)
    for copy in sends:
        copy.wait_send()


def on_device(
    out_grad, route_ids, combine, row_lists, saved_inputs, gate_weight, up_weight, down_weight
):
    n = lax.axis_size("expert")
    chips = n // CORES
    batches = row_lists.shape[0]
    owned, width = out_grad.shape
    rows = owned // batches
    slots = saved_inputs.shape[2]
    hidden = gate_weight.shape[2]
    lanes = max(-(-slots // 128), -(-owned // 128)) * 128
    meta_rows = -(-(1 + batches) // 8) * 8
    splits = [2] * batches
    count = sum(splits)
    hbm = pl.BlockSpec(memory_space=pl.ANY)
    vmem = pl.BlockSpec(memory_space=pltpu.VMEM)
    dma = pltpu.SemaphoreType.DMA
    return pl.pallas_call(
        functools.partial(kernel, n, splits),
        out_shape=jax.ShapeDtypeStruct(out_grad.shape, out_grad.dtype),
        in_specs=[hbm, vmem, vmem, vmem, hbm, hbm, hbm, hbm],
        out_specs=vmem,
        scratch_shapes=[
            pltpu.VMEM((chips, CORES, batches, rows, width), BF16),
            pltpu.VMEM((batches, slots, width), BF16),
            pltpu.VMEM((width, hidden), BF16),
            pltpu.VMEM((width, hidden), BF16),
            pltpu.VMEM((hidden, width), BF16),
            pltpu.VMEM((chips, CORES, meta_rows, lanes), F32),
            pltpu.VMEM((chips, CORES, meta_rows, lanes), F32),
            pltpu.VMEM((batches, n * rows, width), BF16),
            pltpu.VMEM((batches, n * rows, hidden), F32),
            pltpu.VMEM((batches, n * rows, hidden), F32),
            pltpu.VMEM((chips, batches, rows, width), BF16),
            pltpu.VMEM((chips, batches, rows, width), BF16),
            pltpu.VMEM((chips, batches, rows, width), BF16),
            pltpu.VMEM((chips, batches, rows, width), BF16),
            pltpu.VMEM((batches, rows, width), F32),
            pltpu.VMEM((width, hidden), BF16),
            pltpu.VMEM((2 * hidden, width), BF16),
            dma((4 + batches,)),
            dma((chips, CORES)),
            dma((chips, CORES)),
            dma((chips, CORES, count)),
            dma((chips, CORES, count)),
            dma((chips, count)),
            dma((chips, count)),
            dma((chips, count)),
            dma((chips, count)),
        ],
        compiler_params=pltpu.CompilerParams(
            collective_id=0, has_side_effects=True, vmem_limit_bytes=60 * 1024 * 1024
        ),
    )(out_grad, route_ids.T, combine.T, row_lists, saved_inputs, gate_weight, up_weight, down_weight)


def solution(mesh):
    return jax.shard_map(
        on_device,
        mesh=mesh,
        in_specs=(
            P(("dp", "expert"), None),
            P(("dp", "expert"), None),
            P(("dp", "expert"), None),
            P("dp", None, "expert"),
            P("dp", "expert", None, None),
            P("expert", None, None),
            P("expert", None, None),
            P("expert", None, None),
        ),
        out_specs=P(("dp", "expert"), None),
        check_vma=False,
    )
```
